128 devices in a mesh: ctx: 8 (over y_lo, x), tp: 16 (over z, y_hi, core).
Axes of the slice: x: 4, y: 4 (y_hi: 2, y_lo: 2; y = y_hi * 2 + y_lo), z: 4, core: 2. Of those that a mesh axis runs over, the one named last changes fastest.
Arguments:
- inputs: bfloat16 [6144, 4096], P('ctx', 'tp'), may hold values from -6 to 6
- in_proj: bfloat16 [4096, 3, 4096], P(None, None, 'tp'), may hold values from -0.125 to 0.125
- out_proj: bfloat16 [4096, 4096], P('tp'), may hold values from -0.125 to 0.125
- short_taps: float32 [7, 3, 4096], P(None, None, 'tp'), may hold values from -2.4 to 2.4
- skip_gain: float32 [4096], P('tp'), may hold values from -4 to 4
- long_taps: bfloat16 [128, 256], P(None, 'tp'), may hold values from -1 to 1
- cotangent: bfloat16 [6144, 4096], P('ctx', 'tp'), may hold values from -1.5 to 1.5
Outputs:
- layer_out: bfloat16 [6144, 4096], P('ctx', 'tp')
- grad_inputs: bfloat16 [6144, 4096], P('ctx', 'tp')
- grad_in_proj: float32 [4096, 3, 4096], P('ctx', None, 'tp')
- grad_out_proj: float32 [4096, 4096], P('tp', 'ctx')
- grad_long_taps: float32 [128, 256], P(None, 'tp')
The draws below stay inside these ranges and needn't reach their ends.
All inputs are finite; a program needn't handle non-finite values.
Results may differ from the reference program's by a relative error of at most 0.014.
Values may be sent and summed in bfloat16 or wider, within the bound.
A program may use at most 128 MiB of HBM per device.

```python
import jax
import jax.numpy as jnp
from jax import lax

D = 4096
GROUP = 16
LTAPS = 128
STAPS = 7
TOKENS = 6144
GROUPS = 256
N_TP = 16


def draw_long_taps(key, part):
    rate_key = jax.random.fold_in(key, 11)
    value_key = jax.random.fold_in(key, 12)
    rates = jnp.exp(jax.random.uniform(rate_key, (1, GROUPS), jnp.float32, jnp.log(1.0 / 400.0), jnp.log(1.0 / 20.0)))
    values = jnp.clip(jax.random.normal(value_key, (LTAPS, GROUPS), jnp.float32), -6.0, 6.0)
    lag_values = jnp.arange(LTAPS, dtype=jnp.float32)[:, None]
    return (0.15 * values * jnp.exp(-lag_values * rates)).astype(jnp.bfloat16)


def spiked(array, own_key, source, target, blocks, factor):
    def block_of(axis_at):
        return (jnp.arange(array.shape[axis_at]) // (array.shape[axis_at] // blocks)).reshape((-1,) + (1,) * (array.ndim - 1 - axis_at))

    one_side = jax.random.permutation(own_key, blocks)[block_of(target)]
    other_side = (block_of(target) + blocks // 2) % blocks
    return jnp.where((block_of(source) == one_side) | (block_of(source) == other_side), factor * array, array)


def shard_levels(stream_key, shape, shards, low, largest):
    level = 1.0
    for axis_at, blocks in shards:
        steps = jax.random.uniform(jax.random.fold_in(jax.random.fold_in(stream_key, 6), axis_at), (blocks,), jnp.float32, low / len(shards), largest / len(shards))
        level = level * jnp.repeat(jnp.exp(steps), shape[axis_at] // blocks).reshape((-1,) + (1,) * (len(shape) - 1 - axis_at))
    return level


def bell_draw(key, extent, scale, reach, pieces=(), kind=jnp.bfloat16):
    factor_of = shard_levels(key, extent, pieces, -0.22, 0.18) if pieces else 1.0
    result = jax.random.normal(key, extent, jnp.float32) * scale * factor_of
    return jnp.minimum(jnp.maximum(result, -reach), reach).astype(kind)


def noise_with(key, dims, scale, most, split, heavy, kind=jnp.bfloat16):
    values = scale * jax.random.normal(key, dims, jnp.float32)
    if split:
        values = values * shard_levels(key, dims, split, -0.22, 0.18)
    return jnp.clip(spiked(values, jax.random.fold_in(key, 3), *heavy), -most, most).astype(kind)


def setup_inputs(seed: int = 0) -> dict:
    keys = jax.random.split(jax.random.key(seed), 8)
    return {
        "inputs": bell_draw(keys[0], (TOKENS, D), 1.0, 6.0, ((0, 8), (1, 16))),
        "in_proj": noise_with(keys[1], (D, 3, D), D ** -0.5, 0.125, ((2, 16),), (2, 0, 16, 2.0)),
        "out_proj": noise_with(keys[2], (D, D), D ** -0.5, 0.125, ((0, 16),), (0, 1, 16, 2.0)),
        "short_taps": bell_draw(keys[3], (STAPS, 3, D), 0.4, 2.4, ((2, 16),), jnp.float32),
        "skip_gain": bell_draw(keys[4], (D,), 1.0, 4.0, ((0, 16),), jnp.float32),
        "long_taps": draw_long_taps(jax.random.fold_in(keys[7], 71), 0),
        "cotangent": bell_draw(keys[6], (TOKENS, D), 0.25, 1.5, ((0, 8), (1, 16))),
    }


def short_forward(projected, short_taps):
    row_count = projected.shape[0]
    padded = jnp.pad(projected.astype(jnp.float32), ((STAPS - 1, 0), (0, 0), (0, 0)))
    running = jnp.zeros(projected.shape, jnp.float32)
    for lag_index in range(STAPS):
        offset = STAPS - 1 - lag_index
        running = running + short_taps[lag_index] * padded[offset:offset + row_count]
    return running


def short_backward(grad_mixed, short_taps):
    row_count = grad_mixed.shape[0]
    padded = jnp.pad(grad_mixed.astype(jnp.float32), ((0, STAPS - 1), (0, 0), (0, 0)))
    running = jnp.zeros(grad_mixed.shape, jnp.float32)
    for lag_index in range(STAPS):
        running = running + short_taps[lag_index] * padded[lag_index:lag_index + row_count]
    return running


def long_forward(gated, long_taps):
    row_count = gated.shape[0]
    padded = jnp.pad(gated.astype(jnp.float32), ((LTAPS - 1, 0), (0, 0)))
    per_channel = jnp.repeat(long_taps.astype(jnp.float32), GROUP, axis=1)

    def one_tap(lag_index, running):
        piece = lax.dynamic_slice_in_dim(padded, LTAPS - 1 - lag_index, row_count, 0)
        return running + per_channel[lag_index] * piece

    return lax.fori_loop(0, LTAPS, one_tap, jnp.zeros(gated.shape, jnp.float32))


def long_backward(grad_wave, long_taps):
    row_count = grad_wave.shape[0]
    padded = jnp.pad(grad_wave.astype(jnp.float32), ((0, LTAPS - 1), (0, 0)))
    per_channel = jnp.repeat(long_taps.astype(jnp.float32), GROUP, axis=1)

    def one_tap(lag_index, running):
        piece = lax.dynamic_slice_in_dim(padded, lag_index, row_count, 0)
        return running + per_channel[lag_index] * piece

    return lax.fori_loop(0, LTAPS, one_tap, jnp.zeros(grad_wave.shape, jnp.float32))


def tap_gradient(grad_wave, gated):
    row_count = gated.shape[0]
    padded = jnp.pad(gated.astype(jnp.float32), ((LTAPS - 1, 0), (0, 0)))
    grad_float = grad_wave.astype(jnp.float32)

    def one_lag(lag_index):
        piece = lax.dynamic_slice_in_dim(padded, LTAPS - 1 - lag_index, row_count, 0)
        return jnp.sum(grad_float * piece, axis=0).reshape(GROUPS, GROUP).sum(axis=1)

    return lax.map(one_lag, jnp.arange(LTAPS, dtype=jnp.int32))


def blockwise_output(filtered, out_proj):
    block_width = D // N_TP

    def one_block(block_index, running):
        first = (block_index * block_width).astype(jnp.int32)
        left = lax.dynamic_slice_in_dim(filtered, first, block_width, 1)
        right = lax.dynamic_slice_in_dim(out_proj, first, block_width, 0)
        partial_sum = jnp.dot(left, right, preferred_element_type=jnp.float32).astype(jnp.bfloat16)
        return running + partial_sum.astype(jnp.float32)

    start = jnp.zeros((filtered.shape[0], out_proj.shape[1]), jnp.float32)
    return lax.fori_loop(0, N_TP, one_block, start)


def blockwise_inputs(grad_projected, in_proj):
    block_width = D // N_TP
    row_count = grad_projected.shape[0]

    def one_block(block_index, running):
        first = (block_index * block_width).astype(jnp.int32)
        left = lax.dynamic_slice_in_dim(grad_projected, first, block_width, 2).reshape(row_count, 3 * block_width)
        right = lax.dynamic_slice_in_dim(in_proj, first, block_width, 2).reshape(D, 3 * block_width)
        partial_sum = lax.dot_general(left, right, (((1,), (1,)), ((), ())), preferred_element_type=jnp.float32).astype(jnp.bfloat16)
        return running + partial_sum.astype(jnp.float32)

    start = jnp.zeros((row_count, D), jnp.float32)
    return lax.fori_loop(0, N_TP, one_block, start)


def reference(inputs, in_proj, out_proj, short_taps, skip_gain, long_taps, cotangent):
    row_count = inputs.shape[0]
    in_matrix = in_proj.reshape(D, 3 * D)
    projected = jnp.dot(inputs, in_matrix, preferred_element_type=jnp.float32).astype(jnp.bfloat16)
    projected = projected.reshape(row_count, 3, D)
    mixed = short_forward(projected, short_taps)
    query, keyed, valued = mixed[:, 0], mixed[:, 1], mixed[:, 2]
    gated = (keyed * valued).astype(jnp.bfloat16)
    wave = long_forward(gated, long_taps) + skip_gain * gated.astype(jnp.float32)
    filtered = (query * wave).astype(jnp.bfloat16)
    layer_out = blockwise_output(filtered, out_proj).astype(jnp.bfloat16)
    grad_filtered = jnp.dot(cotangent, out_proj.T, preferred_element_type=jnp.float32)
    grad_out_proj = jnp.dot(filtered.T, cotangent, preferred_element_type=jnp.float32)
    grad_wave = (grad_filtered * query).astype(jnp.bfloat16)
    grad_query = grad_filtered * wave
    grad_gated = long_backward(grad_wave, long_taps) + skip_gain * grad_wave.astype(jnp.float32)
    grad_long_taps = tap_gradient(grad_wave, gated)
    grad_mixed = jnp.stack([grad_query, grad_gated * valued, grad_gated * keyed], axis=1).astype(jnp.bfloat16)
    grad_projected = short_backward(grad_mixed, short_taps).astype(jnp.bfloat16)
    grad_matrix = grad_projected.reshape(row_count, 3 * D)
    grad_inputs = blockwise_inputs(grad_projected, in_proj).astype(jnp.bfloat16)
    grad_in_proj = jnp.dot(inputs.T, grad_matrix, preferred_element_type=jnp.float32).reshape(D, 3, D)
    return layer_out, grad_inputs, grad_in_proj, grad_out_proj, grad_long_taps
```

```python
import jax
import jax.numpy as jnp
from jax import lax
from jax.experimental import pallas as pl
from jax.experimental.pallas import tpu as pltpu
from jax.sharding import PartitionSpec as P

GROUP = 16
LTAPS = 128
STAPS = 7
MESH = pl.DeviceIdType.MESH
F32 = jnp.float32
BF16 = jnp.bfloat16
T = 768
C = 256
NT = T // LTAPS
HALF = T // 2


def dot(a, b, dims=((1,), (0,))):
    return lax.dot_general(a, b, (dims, ((), ())), preferred_element_type=F32)


def remote(src, dst, send, recv, where):
    return pltpu.make_async_remote_copy(
        src_ref=src, dst_ref=dst, send_sem=send, recv_sem=recv, device_id=where, device_id_type=MESH
    )


class Gather:
    def __init__(self, src, buf, send, recv, z, h, k):
        self.src, self.buf = src, buf
        zp, zm, zo = lax.rem(z + 1, 4), lax.rem(z + 3, 4), lax.rem(z + 2, 4)

        def at(zz, hh, kk):
            return zz * 4 + hh * 2 + kk

        g, q = 1 - h, 1 - k
        plus, minus = {"tp": at(zp, h, k)}, {"tp": at(zm, h, k)}
        side, mate = {"tp": at(z, g, k)}, {"tp": at(z, h, q)}
        own = at(z, h, k)
        first, second = pl.ds(0, HALF), pl.ds(HALF, HALF)
        whole = pl.ds(0, T)
        plan = [
            (own, whole, plus),
            (own, whole, minus),
            (own, whole, side),
            (own, whole, mate),
            (at(z, g, k), whole, plus),
            (at(z, g, k), whole, minus),
            (at(z, g, k), whole, mate),
            (at(zm, h, k), first, plus),
            (at(zp, h, k), second, minus),
            (at(zm, h, k), whole, mate),
            (at(zp, h, k), whole, mate),
            (at(zm, g, k), first, plus),
            (at(zp, g, k), second, minus),
            (at(zm, g, k), whole, mate),
            (at(zp, g, k), whole, mate),
            (at(zo, h, k), whole, mate),
            (at(zo, g, k), whole, mate),
        ]
        self.copies = []
        for i, (slot, rows, where) in enumerate(plan):
            source = src if i < 4 else buf.at[slot, rows]
            self.copies.append(remote(source, buf.at[slot, rows], send.at[i], recv.at[i], where))
        self.groups = [
            (own, at(z, h, q)),
            (at(zm, h, k), at(zp, h, k)),
            (at(zm, h, q), at(zp, h, q)),
            (at(z, g, k), at(z, g, q)),
            (at(zm, g, k), at(zp, g, k)),
            (at(zm, g, q), at(zp, g, q)),
            (at(zo, h, k), at(zo, h, q)),
            (at(zo, g, k), at(zo, g, q)),
        ]

    def start(self, *which):
        for i in which:
            self.copies[i].start()

    def wait(self, *which):
        for i in which:
            self.copies[i].wait_recv()

    def drain(self):
        for copy in self.copies:
            copy.wait_send()


class Ring:
    def __init__(self, out, inn, side_out, side_in, send, recv, plus, minus, side, part):
        self.out, self.inn, self.side_out, self.side_in = out, inn, side_out, side_in
        self.part = part
        self.copies = []
        for kind in range(2):
            for i, (low, size, where) in enumerate([(0, 1, plus), (1, 1, minus), (2, 2, plus), (4, 2, minus)]):
                span = pl.ds(low, size)
                self.copies.append(
                    remote(out.at[kind, span], inn.at[kind, span], send.at[kind * 4 + i], recv.at[kind * 4 + i], where)
                )
        self.copies.append(remote(side_out, side_in, send.at[8], recv.at[8], side))

    def first(self, kind):
        for half in range(2):
            self.part("o", kind, half, [], self.out.at[kind, half])
            self.copies[kind * 4 + half].start()

    def second(self, kind):
        o, r = self.out, self.inn
        self.copies[kind * 4].wait_recv()
        self.part("p", kind, 0, [r.at[kind, 0]], o.at[kind, 2])
        self.part("p", kind, 1, [], o.at[kind, 3])
        self.copies[kind * 4 + 2].start()
        self.copies[kind * 4 + 1].wait_recv()
        self.part("m", kind, 0, [], o.at[kind, 4])
        self.part("m", kind, 1, [r.at[kind, 1]], o.at[kind, 5])
        self.copies[kind * 4 + 3].start()

    def third(self):
        r = self.inn
        self.copies[6].wait_recv()
        self.copies[7].wait_recv()
        for half in range(2):
            self.part("c", 1, half, [r.at[1, 2 + half], r.at[1, 4 + half]], self.side_out.at[half])
        self.copies[8].start()

    def last(self, targets):
        r = self.inn
        self.copies[2].wait_recv()
        self.copies[3].wait_recv()
        self.copies[8].wait_recv()
        for half in range(2):
            self.part("c", 0, half, [r.at[0, 2 + half], r.at[0, 4 + half], self.side_in.at[half]], targets[half])

    def drain(self):
        for copy in self.copies:
            copy.wait_send()


def body(
    inputs_ref, cot_ref, w_hbm, op_hbm, staps_ref, skip_ref, hrev_ref, hfwd_ref,
    lo_out, gi_out, gin_out, gout_out, taps_out,
    X, Y, W, OP, PF, QKV, WAVE, GF, FIL, FT, GM, GT, GWT, TT, HS, HR, HT, TG, TGR, GOS, LOS, GIS,
    SP, LRP, GRP, S, LR, GR, SY, LRY, GRY, CS, CR, CSY, CRY, OS, OR, OSY, ORY,
    xs, xr, ys, yr, lps, lpr, gps, gpr, ls, lr, gs, gr, cs, cr, os_, or_, hs, hr, ts, tr, loc,
):
    ctx = lax.axis_index("ctx")
    me = lax.axis_index("tp")
    z, h, k = me // 4, lax.rem(me // 2, 2), lax.rem(me, 2)
    l, x = ctx // 4, lax.rem(ctx, 4)

    def at(zz, hh, kk):
        return zz * 4 + hh * 2 + kk

    zp, zm, zo = lax.rem(z + 1, 4), lax.rem(z + 3, 4), lax.rem(z + 2, 4)
    xp, xm, xo = lax.rem(x + 1, 4), lax.rem(x + 3, 4), lax.rem(x + 2, 4)
    mate = {"tp": at(z, h, 1 - k)}

    barrier = pltpu.get_barrier_semaphore()
    peers = [{"tp": at(zp, h, k)}, {"tp": at(zm, h, k)}, {"tp": at(z, 1 - h, k)}, mate]
    peers += [{"ctx": lax.rem(ctx + i, 8)} for i in range(1, 8)]
    for peer in peers:
        pl.semaphore_signal(barrier, inc=1, device_id=peer, device_id_type=MESH)
    pl.semaphore_wait(barrier, len(peers))

    gx = Gather(inputs_ref, X, xs, xr, z, h, k)
    gy = Gather(cot_ref, Y, ys, yr, z, h, k)
    gx.start(2, 0, 1, 3)
    loads = [
        pltpu.make_async_copy(inputs_ref, X.at[me], loc.at[0]),
        pltpu.make_async_copy(w_hbm, W, loc.at[1]),
        pltpu.make_async_copy(op_hbm, OP, loc.at[2]),
        pltpu.make_async_copy(cot_ref, Y.at[me], loc.at[3]),
    ]
    for load in loads:
        load.start()

    def project(index, fresh=False):
        a, b = gx.groups[index]

        def one(s, _):
            for at_half in range(2):
                rows = pl.ds(at_half * HALF, HALF)
                to = pl.ds(8 + at_half * HALF, HALF)
                total = dot(X[a, rows], W[s, pl.ds(pl.multiple_of(a * C, C), C), :])
                total = total + dot(X[b, rows], W[s, pl.ds(pl.multiple_of(b * C, C), C), :])
                PF[s, to, :] = total if fresh else PF[s, to, :] + total
            return 0

        lax.fori_loop(0, 3, one, 0)

    loads[0].wait()
    loads[1].wait()
    gx.wait(3)
    project(0, True)
    gx.wait(0)
    gx.start(7, 9)
    gx.wait(1)
    gx.start(8, 10)
    project(1)
    gx.wait(2)
    gx.start(4, 5, 6)
    gy.start(2)
    gx.wait(9, 10)
    project(2)
    gx.wait(6)
    project(3)
    gx.wait(7, 8)
    gx.start(15)
    gx.wait(4)
    gx.start(11, 13)
    gx.wait(5)
    gx.start(12, 14)
    gy.start(0, 1, 3)
    project(4)
    gx.wait(15)
    project(6)
    gx.wait(13, 14)
    project(5)
    gx.wait(11, 12)
    gx.start(16)
    gx.wait(16)
    project(7)

    def round_rows(i, _):
        s, r = i // NT, lax.rem(i, NT)
        rows = pl.ds(pl.multiple_of(8 + r * LTAPS, 8), LTAPS)
        PF[s, rows, :] = PF[s, rows, :].astype(BF16).astype(F32)
        return 0

    nxt, prv = {"ctx": lax.rem(ctx + 1, 8)}, {"ctx": lax.rem(ctx + 7, 8)}
    for s in range(3):
        HS[0, s] = PF[s, T - 8 : T + 8, :].astype(BF16)
    halo0 = remote(HS.at[0], HR.at[0], hs.at[0], hr.at[0], nxt)
    halo0.start()
    lax.fori_loop(0, 3 * NT, round_rows, 0)
    gy.wait(2)
    gy.start(4, 5, 6)
    gy.wait(0)
    gy.start(7, 9)
    gy.wait(1)
    gy.start(8, 10)
    halo0.wait_recv()
    begins, ends = ctx == 0, ctx == 7
    for s in range(3):
        tail = HR[0, s].astype(F32)[8:16]
        PF[s, 0:8, :] = jnp.where(begins, 0.0, tail)

    def short_forward(i, _):
        s, r = i // NT, lax.rem(i, NT)
        window = PF[s, pl.ds(pl.multiple_of(r * LTAPS, 8), LTAPS + 8), :]
        total = staps_ref[s, 0:1, :] * window[8:]
        for j in range(1, STAPS):
            total = total + staps_ref[s, j : j + 1, :] * pltpu.roll(window, j, 0)[8:]
        QKV[s, pl.ds(pl.multiple_of(r * LTAPS, LTAPS), LTAPS), :] = total
        return 0

    lax.fori_loop(0, 3 * NT, short_forward, 0)

    def tile_rows(n):
        return pl.ds(pl.multiple_of(n * LTAPS, LTAPS), LTAPS)

    def gated_tile(n):
        return (QKV[1, tile_rows(n), :] * QKV[2, tile_rows(n), :]).astype(BF16).astype(F32)

    def put_gated(n, _):
        GT[n + 1] = gated_tile(n).T.astype(BF16)
        return 0

    lax.fori_loop(0, NT, put_gated, 0)
    halo1 = remote(GT.at[NT], HT.at[0], hs.at[1], hr.at[1], nxt)
    halo1.start()
    gy.wait(4)
    gy.start(11, 13)
    gy.wait(5)
    gy.start(12, 14)
    gy.wait(7, 8)
    gy.start(15)
    halo1.wait_recv()
    GT[0] = jnp.where(begins, 0.0, HT[0].astype(F32)).astype(BF16)

    def windows(ref, rows):
        return jnp.concatenate(
            [jnp.concatenate([ref[n, rows, :], ref[n + 1, rows, :]], axis=1) for n in range(NT)], axis=0
        )

    def band_of(ref, g):
        spread = jnp.broadcast_to(ref[g], (LTAPS, 2 * LTAPS))
        return pltpu.roll(spread, 0, 1, stride=1, stride_axis=0).astype(BF16)

    def convolve(g, _):
        rows = pl.ds(pl.multiple_of(g * GROUP, GROUP), GROUP)
        got = dot(windows(GT, rows), band_of(hrev_ref, g), ((1,), (1,)))
        for n in range(NT):
            TT[n, rows, :] = got[n * GROUP : (n + 1) * GROUP]
        return 0

    lax.fori_loop(0, GROUP, convolve, 0)

    for n in range(NT):
        rows = pl.ds(n * LTAPS, LTAPS)
        wave = TT[n].T + skip_ref[...] * gated_tile(n)
        WAVE[rows, :] = wave
        fil = (QKV[0, rows, :] * wave).astype(BF16)
        FIL[rows, :] = fil
        FT[:, rows] = fil.astype(F32).T.astype(BF16)

    def lo_part(slot, half):
        return dot(FIL[pl.ds(half * HALF, HALF), :], OP[:, pl.ds(pl.multiple_of(slot * C, C), C)])

    def gi_part(slot, half):
        rows = pl.ds(half * HALF, HALF)
        picked = pl.ds(pl.multiple_of(slot * C, C), C)
        total = dot(GM[0, rows, :], W[0, picked, :], ((1,), (1,)))
        total = total + dot(GM[1, rows, :], W[1, picked, :], ((1,), (1,)))
        return total + dot(GM[2, rows, :], W[2, picked, :], ((1,), (1,)))

    def for_mate(part, pairs):
        for index, pair in enumerate(pairs):
            def one(half, _, index=index):
                i = index
                zz, hh = (zo, zp, zm, z)[i // 2], (1 - h, h)[i % 2]
                SP[i, half] = part(at(zz, hh, 1 - k), half).astype(BF16)
                return 0

            lax.fori_loop(0, 2, one, 0)
            pair.start()

    def mate_pairs(into, send, recv):
        return [remote(SP.at[i], into.at[i], send.at[i], recv.at[i], mate) for i in range(8)]

    def tp_ring(part, from_mate, pairs, inn, side_in, send, recv):
        def term(name, kind, half, extra, target):
            place = {"o": 0, "p": 1, "m": 2, "c": 3}[name]
            index = place * 2 + (0 if kind == 1 else 1)
            if half == 0:
                pairs[index].wait_recv()
            zz = (zo, zp, zm, z)[place]
            hh = 1 - h if kind == 1 else h
            total = part(at(zz, hh, k), half) + from_mate[index, half].astype(F32)
            for ref in extra:
                total = total + ref[...].astype(F32)
            target[...] = total.astype(target.dtype)

        return Ring(
            S, inn, SY, side_in, send, recv,
            {"tp": at(zp, h, k)}, {"tp": at(zm, h, k)}, {"tp": at(z, 1 - h, k)}, term,
        )

    def ctx_ring(fill, out, inn, side_out, side_in, send, recv):
        def term(name, kind, half, extra, target):
            xx = {"o": xo, "p": xp, "m": xm, "c": x}[name]
            ll = 1 - l if kind == 1 else l
            fill((ll * 4 + xx) * 2 + half, half, extra, target)

        return Ring(
            out, inn, side_out, side_in, send, recv,
            {"ctx": l * 4 + xp}, {"ctx": l * 4 + xm}, {"ctx": (1 - l) * 4 + x}, term,
        )

    loads[2].wait()
    lo_pairs = mate_pairs(LRP, lps, lpr)
    for_mate(lo_part, lo_pairs)

    def filter_grad(index, fresh=False):
        a, b = gy.groups[index]

        def one(i, _):
            rows = pl.ds(pl.multiple_of(i * HALF, HALF), HALF)
            total = dot(Y[a, rows, :], OP[:, pl.ds(pl.multiple_of(a * C, C), C)], ((1,), (1,)))
            total = total + dot(Y[b, rows, :], OP[:, pl.ds(pl.multiple_of(b * C, C), C)], ((1,), (1,)))
            GF[rows, :] = total if fresh else GF[rows, :] + total
            return 0

        lax.fori_loop(0, 2, one, 0)

    loads[3].wait()
    gy.wait(3)
    filter_grad(0, True)
    filter_grad(1)
    gy.wait(9, 10)
    filter_grad(2)
    gy.wait(6)
    filter_grad(3)
    gy.wait(11, 12)
    gy.start(16)
    filter_grad(4)
    gy.wait(15)
    filter_grad(6)
    gy.wait(13, 14)
    filter_grad(5)
    gy.wait(16)
    filter_grad(7)

    def put_grad_wave(n, _):
        rows = tile_rows(n)
        GWT[n] = (GF[rows, :] * QKV[0, rows, :]).astype(BF16).astype(F32).T.astype(BF16)
        return 0

    lax.fori_loop(0, NT, put_grad_wave, 0)
    halo2 = remote(GWT.at[0], HT.at[1], hs.at[2], hr.at[2], prv)
    halo2.start()

    def go_fill(slot, half, extra, target):
        total = dot(FT[...], Y[slot])
        for ref in extra:
            total = total + ref[0].astype(F32)
        target[0] = total.astype(target.dtype)

    go = ctx_ring(go_fill, OS, OR, OSY, ORY, os_, or_)
    go.first(1)
    go.first(0)
    lo = tp_ring(lo_part, LRP, lo_pairs, LR, LRY, ls, lr)
    lo.first(1)
    lo.first(0)

    halo2.wait_recv()
    GWT[NT] = jnp.where(ends, 0.0, HT[1].astype(F32)).astype(BF16)

    def convolve_back(g, _):
        rows = pl.ds(pl.multiple_of(g * GROUP, GROUP), GROUP)
        got = dot(windows(GWT, rows), band_of(hfwd_ref, g), ((1,), (1,)))
        for n in range(NT):
            TT[n, rows, :] = got[n * GROUP : (n + 1) * GROUP]
        return 0

    lax.fori_loop(0, GROUP, convolve_back, 0)

    def to_mixed(n, _):
        rows = tile_rows(n)
        gf, q = GF[rows, :], QKV[0, rows, :]
        gw = (gf * q).astype(BF16).astype(F32)
        gg = TT[n].T + skip_ref[...] * gw
        PF[0, rows, :] = (gf * WAVE[rows, :]).astype(BF16).astype(F32)
        PF[1, rows, :] = (gg * QKV[2, rows, :]).astype(BF16).astype(F32)
        PF[2, rows, :] = (gg * QKV[1, rows, :]).astype(BF16).astype(F32)
        return 0

    lax.fori_loop(0, NT, to_mixed, 0)
    for s in range(3):
        HS[1, s] = PF[s, 0:16, :].astype(BF16)
    halo3 = remote(HS.at[1], HR.at[1], hs.at[3], hr.at[3], prv)
    halo3.start()

    def correlate(g, _):
        rows = pl.ds(pl.multiple_of(g * GROUP, GROUP), GROUP)
        now = jnp.concatenate([GWT[n, rows, :] for n in range(NT)], axis=0)
        across = lax.broadcasted_iota(jnp.int32, (LTAPS, LTAPS), 0) + lax.broadcasted_iota(jnp.int32, (LTAPS, LTAPS), 1)
        mirror = jnp.where(across == LTAPS - 1, 1.0, 0.0).astype(BF16)
        tiles = [dot(GT[n, rows, :], mirror).astype(BF16) for n in range(NT + 1)]
        seen = jnp.concatenate(
            [jnp.concatenate([tiles[n + 1], tiles[n]], axis=1) for n in range(NT)], axis=0
        )
        pairs = dot(now, seen, ((0,), (0,)))
        TG[g] = jnp.sum(pltpu.roll(pairs, LTAPS + 1, 1, stride=1, stride_axis=0)[:, :LTAPS], axis=0, keepdims=True)
        return 0

    go.second(1)
    halo3.wait_recv()
    for s in range(3):
        head = HR[1, s].astype(F32)[0:8]
        PF[s, T : T + 8, :] = jnp.where(ends, 0.0, head)

    def short_backward(i, _):
        s, r = i // NT, lax.rem(i, NT)
        window = PF[s, pl.ds(pl.multiple_of(r * LTAPS, 8), LTAPS + 8), :]
        total = staps_ref[s, 0:1, :] * window[:LTAPS]
        for j in range(1, STAPS):
            total = total + staps_ref[s, j : j + 1, :] * pltpu.roll(window, LTAPS + 8 - j, 0)[:LTAPS]
        GM[s, pl.ds(pl.multiple_of(r * LTAPS, LTAPS), LTAPS), :] = total.astype(BF16)
        return 0

    lax.fori_loop(0, 3 * NT, short_backward, 0)

    def gin_fill(slot, half, extra, target):
        flipped = X[slot]

        def one(s, _):
            total = dot(flipped, GM[s], ((0,), (0,)))
            for ref in extra:
                total = total + ref[s].astype(F32)
            target[s] = total.astype(target.dtype)
            return 0

        lax.fori_loop(0, 3, one, 0)

    gin = ctx_ring(gin_fill, CS, CR, CSY, CRY, cs, cr)
    gin.first(1)
    go.second(0)
    gin.first(0)
    lo.second(1)
    lo.second(0)
    for pair in lo_pairs:
        pair.wait_send()
    gi_pairs = mate_pairs(GRP, gps, gpr)
    for_mate(gi_part, gi_pairs)
    lax.fori_loop(0, GROUP, correlate, 0)
    tap_sends = []
    for i in range(7):
        tap_sends.append(remote(TG, TGR.at[i], ts.at[i], tr.at[i], {"ctx": lax.rem(ctx + i + 1, 8)}))
        tap_sends[-1].start()
    gin.second(1)
    go.third()
    lo.third()
    gin.second(0)
    lo.last([LOS.at[pl.ds(0, HALF)], LOS.at[pl.ds(HALF, HALF)]])
    lo_store = pltpu.make_async_copy(LOS, lo_out, loc.at[4])
    lo_store.start()
    lo.drain()
    gi = tp_ring(gi_part, GRP, gi_pairs, GR, GRY, gs, gr)
    gi.first(1)
    gi.first(0)
    go.last([GOS.at[:, :, pl.ds(0, C)], GOS.at[:, :, pl.ds(C, C)]])
    go_store = pltpu.make_async_copy(GOS.at[0], gout_out, loc.at[5])
    go_store.start()
    gi.second(1)
    gi.second(0)
    total = TG[...]
    for i in range(7):
        tap_sends[i].wait_recv()
        total = total + TGR[i]
    for i in range(7):
        tap_sends[i].wait_send()
    TG[...] = total
    tap_store = pltpu.make_async_copy(TG, taps_out, loc.at[6])
    tap_store.start()
    gi.third()
    gin.third()
    gi.last([GIS.at[pl.ds(0, HALF)], GIS.at[pl.ds(HALF, HALF)]])
    gi_store = pltpu.make_async_copy(GIS, gi_out, loc.at[7])
    gi_store.start()
    gin.last([PF.at[:, pl.ds(0, C)], PF.at[:, pl.ds(C, C)]])
    gin_store = pltpu.make_async_copy(PF.at[:, pl.ds(0, 2 * C)], gin_out, loc.at[8])
    gin_store.start()

    gx.drain()
    gy.drain()
    go.drain()
    gi.drain()
    gin.drain()
    for pair in gi_pairs:
        pair.wait_send()
    for copy in (halo0, halo1, halo2, halo3):
        copy.wait_send()
    for store in (lo_store, go_store, tap_store, gi_store, gin_store):
        store.wait()


def local(inputs, in_proj, out_proj, short_taps, skip_gain, long_taps, cotangent):
    d = in_proj.shape[0]
    n_tp = d // C
    w = jnp.transpose(in_proj, (1, 0, 2))
    staps = jnp.transpose(short_taps, (1, 0, 2))
    taps = long_taps.astype(F32).T
    zeros = jnp.zeros((GROUP, LTAPS), F32)
    hfwd = jnp.concatenate([taps, zeros], axis=1).reshape(GROUP, 1, 2 * LTAPS)
    hrev = jnp.concatenate([zeros[:, :1], taps[:, ::-1], zeros[:, 1:]], axis=1).reshape(GROUP, 1, 2 * LTAPS)
    vm = pltpu.VMEM
    sem = pltpu.SemaphoreType.DMA
    scratch = [
        vm((n_tp, T, C), BF16), vm((n_tp, T, C), BF16), vm((3, d, C), BF16), vm((C, d), BF16),
        vm((3, T + 8, C), F32), vm((3, T, C), F32), vm((T, C), F32), vm((T, C), F32),
        vm((T, C), BF16), vm((C, T), BF16), vm((3, T, C), BF16),
        vm((NT + 1, C, LTAPS), BF16), vm((NT + 1, C, LTAPS), BF16), vm((NT, C, LTAPS), F32),
        vm((2, 3, 16, C), BF16), vm((2, 3, 16, C), BF16), vm((2, C, LTAPS), BF16),
        vm((GROUP, 1, LTAPS), F32), vm((7, GROUP, 1, LTAPS), F32),
        vm((1, C, 2 * C), F32), vm((T, C), BF16), vm((T, C), BF16),
        vm((8, 2, HALF, C), BF16), vm((8, 2, HALF, C), BF16), vm((8, 2, HALF, C), BF16),
        vm((2, 6, HALF, C), BF16), vm((2, 6, HALF, C), BF16), vm((2, 6, HALF, C), BF16),
        vm((2, HALF, C), BF16), vm((2, HALF, C), BF16), vm((2, HALF, C), BF16),
        vm((2, 6, 3, C, C), BF16), vm((2, 6, 3, C, C), BF16), vm((2, 3, C, C), BF16), vm((2, 3, C, C), BF16),
        vm((2, 6, 1, C, C), BF16), vm((2, 6, 1, C, C), BF16), vm((2, 1, C, C), BF16), vm((2, 1, C, C), BF16),
        sem((17,)), sem((17,)), sem((17,)), sem((17,)),
        sem((8,)), sem((8,)), sem((8,)), sem((8,)),
        sem((9,)), sem((9,)), sem((9,)), sem((9,)),
        sem((9,)), sem((9,)), sem((9,)), sem((9,)),
        sem((4,)), sem((4,)), sem((7,)), sem((7,)), sem((9,)),
    ]
    hbm = pl.BlockSpec(memory_space=pl.ANY)
    vmem = pl.BlockSpec(memory_space=pltpu.VMEM)
    layer_out, grad_inputs, grad_in, grad_out, tap_rows = pl.pallas_call(
        body,
        out_shape=[
            jax.ShapeDtypeStruct((T, C), BF16),
            jax.ShapeDtypeStruct((T, C), BF16),
            jax.ShapeDtypeStruct((3, 2 * C, C), F32),
            jax.ShapeDtypeStruct((C, 2 * C), F32),
            jax.ShapeDtypeStruct((GROUP, 1, LTAPS), F32),
        ],
        in_specs=[hbm, hbm, hbm, hbm, vmem, vmem, vmem, vmem],
        out_specs=[hbm] * 5,
        scratch_shapes=scratch,
        compiler_params=pltpu.CompilerParams(
            collective_id=0, has_side_effects=True, vmem_limit_bytes=67043328
        ),
    )(inputs, cotangent, w, out_proj, staps, skip_gain.reshape(1, C), hrev, hfwd)
    grad_taps = tap_rows.reshape(GROUP, LTAPS).T
    return (layer_out, grad_inputs, jnp.transpose(grad_in, (1, 0, 2)), grad_out, grad_taps)


def solution(mesh):
    placed = (
        P("ctx", "tp"),
        P(None, None, "tp"),
        P("tp", None),
        P(None, None, "tp"),
        P("tp"),
        P(None, "tp"),
        P("ctx", "tp"),
    )
    return jax.shard_map(
        local,
        mesh=mesh,
        in_specs=placed,
        out_specs=(
            P("ctx", "tp"),
            P("ctx", "tp"),
            P("ctx", None, "tp"),
            P("tp", "ctx"),
            P(None, "tp"),
        ),
        check_vma=False,
    )
```

```python
import jax
import jax.numpy as jnp
from jax import lax
from jax.experimental import pallas as pl
from jax.experimental.pallas import tpu as pltpu
from jax.sharding import PartitionSpec as P

GROUP = 16
LTAPS = 128
STAPS = 7
MESH = pl.DeviceIdType.MESH
F32 = jnp.float32
BF16 = jnp.bfloat16
T = 768
C = 256
NT = T // LTAPS
HALF = T // 2


def dot(a, b, dims=((1,), (0,))):
    return lax.dot_general(a, b, (dims, ((), ())), preferred_element_type=F32)


def remote(src, dst, send, recv, where):
    return pltpu.make_async_remote_copy(
        src_ref=src, dst_ref=dst, send_sem=send, recv_sem=recv, device_id=where, device_id_type=MESH
    )


class Gather:
    def __init__(self, src, buf, send, recv, z, h, k):
        self.src, self.buf = src, buf
        zp, zm, zo = lax.rem(z + 1, 4), lax.rem(z + 3, 4), lax.rem(z + 2, 4)

        def at(zz, hh, kk):
            return zz * 4 + hh * 2 + kk

        g, q = 1 - h, 1 - k
        plus, minus = {"tp": at(zp, h, k)}, {"tp": at(zm, h, k)}
        side, mate = {"tp": at(z, g, k)}, {"tp": at(z, h, q)}
        own = at(z, h, k)
        first, second = pl.ds(0, HALF), pl.ds(HALF, HALF)
        whole = pl.ds(0, T)
        plan = [
            (own, whole, plus),
            (own, whole, minus),
            (own, whole, side),
            (own, whole, mate),
            (at(z, g, k), whole, plus),
            (at(z, g, k), whole, minus),
            (at(z, g, k), whole, mate),
            (at(zm, h, k), first, plus),
            (at(zp, h, k), second, minus),
            (at(zm, h, k), whole, mate),
            (at(zp, h, k), whole, mate),
            (at(zm, g, k), first, plus),
            (at(zp, g, k), second, minus),
            (at(zm, g, k), whole, mate),
            (at(zp, g, k), whole, mate),
            (at(zo, h, k), whole, mate),
            (at(zo, g, k), whole, mate),
        ]
        self.copies = []
        for i, (slot, rows, where) in enumerate(plan):
            source = src if i < 4 else buf.at[slot, rows]
            self.copies.append(remote(source, buf.at[slot, rows], send.at[i], recv.at[i], where))
        self.groups = [
            (own, at(z, h, q)),
            (at(zm, h, k), at(zp, h, k)),
            (at(zm, h, q), at(zp, h, q)),
            (at(z, g, k), at(z, g, q)),
            (at(zm, g, k), at(zp, g, k)),
            (at(zm, g, q), at(zp, g, q)),
            (at(zo, h, k), at(zo, h, q)),
            (at(zo, g, k), at(zo, g, q)),
        ]

    def start(self, *which):
        for i in which:
            self.copies[i].start()

    def wait(self, *which):
        for i in which:
            self.copies[i].wait_recv()

    def drain(self):
        for copy in self.copies:
            copy.wait_send()


class Ring:
    def __init__(self, out, inn, side_out, side_in, send, recv, plus, minus, side, part):
        self.out, self.inn, self.side_out, self.side_in = out, inn, side_out, side_in
        self.part = part
        self.copies = []
        for kind in range(2):
            for i, (low, size, where) in enumerate([(0, 1, plus), (1, 1, minus), (2, 2, plus), (4, 2, minus)]):
                span = pl.ds(low, size)
                self.copies.append(
                    remote(out.at[kind, span], inn.at[kind, span], send.at[kind * 4 + i], recv.at[kind * 4 + i], where)
                )
        self.copies.append(remote(side_out, side_in, send.at[8], recv.at[8], side))

    def first(self, kind):
        for half in range(2):
            self.part("o", kind, half, [], self.out.at[kind, half])
            self.copies[kind * 4 + half].start()

    def second(self, kind):
        o, r = self.out, self.inn
        self.copies[kind * 4].wait_recv()
        self.part("p", kind, 0, [r.at[kind, 0]], o.at[kind, 2])
        self.part("p", kind, 1, [], o.at[kind, 3])
        self.copies[kind * 4 + 2].start()
        self.copies[kind * 4 + 1].wait_recv()
        self.part("m", kind, 0, [], o.at[kind, 4])
        self.part("m", kind, 1, [r.at[kind, 1]], o.at[kind, 5])
        self.copies[kind * 4 + 3].start()

    def third(self):
        r = self.inn
        self.copies[6].wait_recv()
        self.copies[7].wait_recv()
        for half in range(2):
            self.part("c", 1, half, [r.at[1, 2 + half], r.at[1, 4 + half]], self.side_out.at[half])
        self.copies[8].start()

    def last(self, targets):
        r = self.inn
        self.copies[2].wait_recv()
        self.copies[3].wait_recv()
        self.copies[8].wait_recv()
        for half in range(2):
            self.part("c", 0, half, [r.at[0, 2 + half], r.at[0, 4 + half], self.side_in.at[half]], targets[half])

    def sent(self, *which):
        for i in which:
            self.copies[i].wait_send()

    def drain(self):
        for copy in self.copies:
            copy.wait_send()


def body(
    inputs_ref, cot_ref, w_hbm, op_hbm, staps_ref, skip_ref, hrev_ref, hfwd_ref,
    lo_out, gi_out, gin_out, gout_out, taps_out,
    X, Y, W, OP, PF, QKV, WAVE, GF, FIL, FT, GM, GT, GWT, TT, HS, HR, HT, TG, TGR, GOS, LOS, GIS,
    SP, LRP, GRP, S, LR, GR, SY, LRY, GRY, CS, CR, CSY, CRY, OS, OR, OSY, ORY,
    xs, xr, ys, yr, lps, lpr, gps, gpr, ls, lr, gs, gr, cs, cr, os_, or_, hs, hr, ts, tr, loc,
):
    ctx = lax.axis_index("ctx")
    me = lax.axis_index("tp")
    z, h, k = me // 4, lax.rem(me // 2, 2), lax.rem(me, 2)
    l, x = ctx // 4, lax.rem(ctx, 4)

    def at(zz, hh, kk):
        return zz * 4 + hh * 2 + kk

    zp, zm, zo = lax.rem(z + 1, 4), lax.rem(z + 3, 4), lax.rem(z + 2, 4)
    xp, xm, xo = lax.rem(x + 1, 4), lax.rem(x + 3, 4), lax.rem(x + 2, 4)
    mate = {"tp": at(z, h, 1 - k)}

    barrier = pltpu.get_barrier_semaphore()
    peers = [{"tp": at(zp, h, k)}, {"tp": at(zm, h, k)}, {"tp": at(z, 1 - h, k)}, mate]
    peers += [{"ctx": lax.rem(ctx + i, 8)} for i in range(1, 8)]
    for peer in peers:
        pl.semaphore_signal(barrier, inc=1, device_id=peer, device_id_type=MESH)
    pl.semaphore_wait(barrier, len(peers))

    gx = Gather(inputs_ref, X, xs, xr, z, h, k)
    gy = Gather(cot_ref, Y, ys, yr, z, h, k)
    gx.start(2, 0, 1, 3)
    gy.start(2)
    loads = [
        pltpu.make_async_copy(inputs_ref, X.at[me], loc.at[0]),
        pltpu.make_async_copy(w_hbm, W, loc.at[1]),
        pltpu.make_async_copy(op_hbm, OP, loc.at[2]),
        pltpu.make_async_copy(cot_ref, Y.at[me], loc.at[3]),
    ]
    for load in loads:
        load.start()

    def project(index, fresh=False):
        a, b = gx.groups[index]

        def one(s, _):
            for at_half in range(2):
                rows = pl.ds(at_half * HALF, HALF)
                to = pl.ds(8 + at_half * HALF, HALF)
                total = dot(X[a, rows], W[s, pl.ds(pl.multiple_of(a * C, C), C), :])
                total = total + dot(X[b, rows], W[s, pl.ds(pl.multiple_of(b * C, C), C), :])
                PF[s, to, :] = total if fresh else PF[s, to, :] + total
            return 0

        lax.fori_loop(0, 3, one, 0)

    loads[0].wait()
    loads[1].wait()
    gx.wait(3)
    project(0, True)
    gx.wait(0)
    gx.start(7, 9)
    gx.wait(1)
    gx.start(8, 10)
    gy.start(0, 1, 3)
    project(1)
    gx.wait(9, 10)
    project(2)
    gx.wait(7, 8)
    gx.start(15)
    gx.wait(2)
    gx.start(4, 5, 6)
    gx.wait(15)
    project(6)
    gx.wait(6)
    project(3)
    gx.wait(4)
    gx.start(11, 13)
    gx.wait(5)
    gx.start(12, 14)
    gy.wait(0, 1)
    gy.start(7, 9, 8, 10)
    project(4)
    gy.wait(2)
    gy.start(4, 5, 6)
    gx.wait(13, 14)
    project(5)
    gx.wait(11, 12)
    gx.start(16)
    gx.wait(16)
    project(7)

    def round_rows(i, _):
        s, r = i // NT, lax.rem(i, NT)
        rows = pl.ds(pl.multiple_of(8 + r * LTAPS, 8), LTAPS)
        PF[s, rows, :] = PF[s, rows, :].astype(BF16).astype(F32)
        return 0

    nxt, prv = {"ctx": lax.rem(ctx + 1, 8)}, {"ctx": lax.rem(ctx + 7, 8)}
    for s in range(3):
        HS[0, s] = PF[s, T - 8 : T + 8, :].astype(BF16)
    halo0 = remote(HS.at[0], HR.at[0], hs.at[0], hr.at[0], nxt)
    halo0.start()
    lax.fori_loop(0, 3 * NT, round_rows, 0)
    halo0.wait_recv()
    begins, ends = ctx == 0, ctx == 7
    for s in range(3):
        tail = HR[0, s].astype(F32)[8:16]
        PF[s, 0:8, :] = jnp.where(begins, 0.0, tail)

    def short_forward(i, _):
        s, r = i // NT, lax.rem(i, NT)
        window = PF[s, pl.ds(pl.multiple_of(r * LTAPS, 8), LTAPS + 8), :]
        total = staps_ref[s, 0:1, :] * window[8:]
        for j in range(1, STAPS):
            total = total + staps_ref[s, j : j + 1, :] * pltpu.roll(window, j, 0)[8:]
        QKV[s, pl.ds(pl.multiple_of(r * LTAPS, LTAPS), LTAPS), :] = total
        return 0

    lax.fori_loop(0, 3 * NT, short_forward, 0)

    def tile_rows(n):
        return pl.ds(pl.multiple_of(n * LTAPS, LTAPS), LTAPS)

    def gated_tile(n):
        return (QKV[1, tile_rows(n), :] * QKV[2, tile_rows(n), :]).astype(BF16).astype(F32)

    def put_gated(n, _):
        GT[n + 1] = gated_tile(n).T.astype(BF16)
        return 0

    lax.fori_loop(0, NT, put_gated, 0)
    halo1 = remote(GT.at[NT], HT.at[0], hs.at[1], hr.at[1], nxt)
    halo1.start()
    gy.wait(7, 8)
    gy.start(15)
    halo1.wait_recv()
    GT[0] = jnp.where(begins, 0.0, HT[0].astype(F32)).astype(BF16)

    def windows(ref, rows):
        return jnp.concatenate(
            [jnp.concatenate([ref[n, rows, :], ref[n + 1, rows, :]], axis=1) for n in range(NT)], axis=0
        )

    def band_of(ref, g):
        spread = jnp.broadcast_to(ref[g], (LTAPS, 2 * LTAPS))
        return pltpu.roll(spread, 0, 1, stride=1, stride_axis=0).astype(BF16)

    def convolve(g, _):
        rows = pl.ds(pl.multiple_of(g * GROUP, GROUP), GROUP)
        got = dot(windows(GT, rows), band_of(hrev_ref, g), ((1,), (1,)))
        for n in range(NT):
            TT[n, rows, :] = got[n * GROUP : (n + 1) * GROUP]
        return 0

    lax.fori_loop(0, GROUP, convolve, 0)
    gy.wait(4)
    gy.start(11, 13)
    gy.wait(5)
    gy.start(12, 14)

    for n in range(NT):
        rows = pl.ds(n * LTAPS, LTAPS)
        wave = TT[n].T + skip_ref[...] * gated_tile(n)
        WAVE[rows, :] = wave
        fil = (QKV[0, rows, :] * wave).astype(BF16)
        FIL[rows, :] = fil
        FT[:, rows] = fil.astype(F32).T.astype(BF16)

    def lo_part(slot, half):
        return dot(FIL[pl.ds(half * HALF, HALF), :], OP[:, pl.ds(pl.multiple_of(slot * C, C), C)])

    def gi_part(slot, half):
        rows = pl.ds(half * HALF, HALF)
        picked = pl.ds(pl.multiple_of(slot * C, C), C)
        total = dot(GM[0, rows, :], W[0, picked, :], ((1,), (1,)))
        total = total + dot(GM[1, rows, :], W[1, picked, :], ((1,), (1,)))
        return total + dot(GM[2, rows, :], W[2, picked, :], ((1,), (1,)))

    def for_mate(part, pairs):
        for index, pair in enumerate(pairs):
            def one(half, _, index=index):
                i = index
                zz, hh = (zo, zp, zm, z)[i // 2], (1 - h, h)[i % 2]
                SP[i, half] = part(at(zz, hh, 1 - k), half).astype(BF16)
                return 0

            lax.fori_loop(0, 2, one, 0)
            pair.start()

    def mate_pairs(into, send, recv):
        return [remote(SP.at[i], into.at[i], send.at[i], recv.at[i], mate) for i in range(8)]

    def tp_ring(part, from_mate, pairs, inn, side_in, send, recv):
        def term(name, kind, half, extra, target):
            place = {"o": 0, "p": 1, "m": 2, "c": 3}[name]
            index = place * 2 + (0 if kind == 1 else 1)
            if half == 0:
                pairs[index].wait_recv()
            zz = (zo, zp, zm, z)[place]
            hh = 1 - h if kind == 1 else h
            total = part(at(zz, hh, k), half) + from_mate[index, half].astype(F32)
            for ref in extra:
                total = total + ref[...].astype(F32)
            target[...] = total.astype(target.dtype)

        return Ring(
            S, inn, SY, side_in, send, recv,
            {"tp": at(zp, h, k)}, {"tp": at(zm, h, k)}, {"tp": at(z, 1 - h, k)}, term,
        )

    def ctx_ring(fill, out, inn, side_out, side_in, send, recv):
        def term(name, kind, half, extra, target):
            xx = {"o": xo, "p": xp, "m": xm, "c": x}[name]
            ll = 1 - l if kind == 1 else l
            fill((ll * 4 + xx) * 2 + half, half, extra, target)

        return Ring(
            out, inn, side_out, side_in, send, recv,
            {"ctx": l * 4 + xp}, {"ctx": l * 4 + xm}, {"ctx": (1 - l) * 4 + x}, term,
        )

    loads[2].wait()
    lo_pairs = mate_pairs(LRP, lps, lpr)
    for_mate(lo_part, lo_pairs)

    def filter_grad(index, fresh=False):
        a, b = gy.groups[index]

        def one(i, _):
            rows = pl.ds(pl.multiple_of(i * HALF, HALF), HALF)
            total = dot(Y[a, rows, :], OP[:, pl.ds(pl.multiple_of(a * C, C), C)], ((1,), (1,)))
            total = total + dot(Y[b, rows, :], OP[:, pl.ds(pl.multiple_of(b * C, C), C)], ((1,), (1,)))
            GF[rows, :] = total if fresh else GF[rows, :] + total
            return 0

        lax.fori_loop(0, 2, one, 0)

    loads[3].wait()
    gy.wait(3)
    filter_grad(0, True)
    filter_grad(1)
    gy.wait(9, 10)
    filter_grad(2)
    gy.wait(6)
    filter_grad(3)
    filter_grad(4)
    gy.wait(15)
    filter_grad(6)
    gy.wait(13, 14)
    filter_grad(5)
    lo = tp_ring(lo_part, LRP, lo_pairs, LR, LRY, ls, lr)
    lo.first(1)
    lo.first(0)
    gy.wait(11, 12)
    gy.start(16)
    gy.wait(16)
    filter_grad(7)

    def put_grad_wave(n, _):
        rows = tile_rows(n)
        GWT[n] = (GF[rows, :] * QKV[0, rows, :]).astype(BF16).astype(F32).T.astype(BF16)
        return 0

    lax.fori_loop(0, NT, put_grad_wave, 0)
    halo2 = remote(GWT.at[0], HT.at[1], hs.at[2], hr.at[2], prv)
    halo2.start()

    def go_fill(slot, half, extra, target):
        total = dot(FT[...], Y[slot])
        for ref in extra:
            total = total + ref[0].astype(F32)
        target[0] = total.astype(target.dtype)

    go = ctx_ring(go_fill, OS, OR, OSY, ORY, os_, or_)
    go.first(1)
    go.first(0)

    halo2.wait_recv()
    GWT[NT] = jnp.where(ends, 0.0, HT[1].astype(F32)).astype(BF16)

    def convolve_back(g, _):
        rows = pl.ds(pl.multiple_of(g * GROUP, GROUP), GROUP)
        got = dot(windows(GWT, rows), band_of(hfwd_ref, g), ((1,), (1,)))
        for n in range(NT):
            TT[n, rows, :] = got[n * GROUP : (n + 1) * GROUP]
        return 0

    lax.fori_loop(0, GROUP, convolve_back, 0)

    def to_mixed(n, _):
        rows = tile_rows(n)
        gf, q = GF[rows, :], QKV[0, rows, :]
        gw = (gf * q).astype(BF16).astype(F32)
        gg = TT[n].T + skip_ref[...] * gw
        PF[0, rows, :] = (gf * WAVE[rows, :]).astype(BF16).astype(F32)
        PF[1, rows, :] = (gg * QKV[2, rows, :]).astype(BF16).astype(F32)
        PF[2, rows, :] = (gg * QKV[1, rows, :]).astype(BF16).astype(F32)
        return 0

    lax.fori_loop(0, NT, to_mixed, 0)
    for s in range(3):
        HS[1, s] = PF[s, 0:16, :].astype(BF16)
    halo3 = remote(HS.at[1], HR.at[1], hs.at[3], hr.at[3], prv)
    halo3.start()
    lo.second(1)
    lo.second(0)

    def correlate(g, _):
        rows = pl.ds(pl.multiple_of(g * GROUP, GROUP), GROUP)
        now = jnp.concatenate([GWT[n, rows, :] for n in range(NT)], axis=0)
        across = lax.broadcasted_iota(jnp.int32, (LTAPS, LTAPS), 0) + lax.broadcasted_iota(jnp.int32, (LTAPS, LTAPS), 1)
        mirror = jnp.where(across == LTAPS - 1, 1.0, 0.0).astype(BF16)
        tiles = [dot(GT[n, rows, :], mirror).astype(BF16) for n in range(NT + 1)]
        seen = jnp.concatenate(
            [jnp.concatenate([tiles[n + 1], tiles[n]], axis=1) for n in range(NT)], axis=0
        )
        pairs = dot(now, seen, ((0,), (0,)))
        TG[g] = jnp.sum(pltpu.roll(pairs, LTAPS + 1, 1, stride=1, stride_axis=0)[:, :LTAPS], axis=0, keepdims=True)
        return 0

    go.second(1)
    halo3.wait_recv()
    for s in range(3):
        head = HR[1, s].astype(F32)[0:8]
        PF[s, T : T + 8, :] = jnp.where(ends, 0.0, head)

    def short_backward(i, _):
        s, r = i // NT, lax.rem(i, NT)
        window = PF[s, pl.ds(pl.multiple_of(r * LTAPS, 8), LTAPS + 8), :]
        total = staps_ref[s, 0:1, :] * window[:LTAPS]
        for j in range(1, STAPS):
            total = total + staps_ref[s, j : j + 1, :] * pltpu.roll(window, LTAPS + 8 - j, 0)[:LTAPS]
        GM[s, pl.ds(pl.multiple_of(r * LTAPS, LTAPS), LTAPS), :] = total.astype(BF16)
        return 0

    lax.fori_loop(0, 3 * NT, short_backward, 0)

    def gin_fill(slot, half, extra, target):
        flipped = X[slot]

        def one(s, _):
            total = dot(flipped, GM[s], ((0,), (0,)))
            for ref in extra:
                total = total + ref[s].astype(F32)
            target[s] = total.astype(target.dtype)
            return 0

        lax.fori_loop(0, 3, one, 0)

    gin = ctx_ring(gin_fill, CS, CR, CSY, CRY, cs, cr)
    gin.first(1)
    gin.first(0)
    go.second(0)
    for pair in lo_pairs:
        pair.wait_send()
    gi_pairs = mate_pairs(GRP, gps, gpr)
    for_mate(gi_part, gi_pairs)
    lo.third()
    go.third()
    gi = tp_ring(gi_part, GRP, gi_pairs, GR, GRY, gs, gr)
    lo.sent(4, 5)
    gi.first(1)
    lo.sent(0, 1)
    gi.first(0)
    gin.second(1)
    lo.sent(6, 7)
    gi.second(1)
    gin.second(0)
    lo.sent(2, 3)
    gi.second(0)
    lax.fori_loop(0, GROUP, correlate, 0)
    tap_sends = []
    for i in range(7):
        tap_sends.append(remote(TG, TGR.at[i], ts.at[i], tr.at[i], {"ctx": lax.rem(ctx + i + 1, 8)}))
        tap_sends[-1].start()
    lo.sent(8)
    gi.third()
    lo.last([LOS.at[pl.ds(0, HALF)], LOS.at[pl.ds(HALF, HALF)]])
    lo_store = pltpu.make_async_copy(LOS, lo_out, loc.at[4])
    lo_store.start()
    go.last([GOS.at[:, :, pl.ds(0, C)], GOS.at[:, :, pl.ds(C, C)]])
    go_store = pltpu.make_async_copy(GOS.at[0], gout_out, loc.at[5])
    go_store.start()
    gin.third()
    total = TG[...]
    for i in range(7):
        tap_sends[i].wait_recv()
        total = total + TGR[i]
    for i in range(7):
        tap_sends[i].wait_send()
    TG[...] = total
    tap_store = pltpu.make_async_copy(TG, taps_out, loc.at[6])
    tap_store.start()
    gi.last([GIS.at[pl.ds(0, HALF)], GIS.at[pl.ds(HALF, HALF)]])
    gi_store = pltpu.make_async_copy(GIS, gi_out, loc.at[7])
    gi_store.start()
    gin.last([PF.at[:, pl.ds(0, C)], PF.at[:, pl.ds(C, C)]])
    gin_store = pltpu.make_async_copy(PF.at[:, pl.ds(0, 2 * C)], gin_out, loc.at[8])
    gin_store.start()

    gx.drain()
    gy.drain()
    go.drain()
    gi.drain()
    gin.drain()
    for pair in gi_pairs:
        pair.wait_send()
    for copy in (halo0, halo1, halo2, halo3):
        copy.wait_send()
    for store in (lo_store, go_store, tap_store, gi_store, gin_store):
        store.wait()


def local(inputs, in_proj, out_proj, short_taps, skip_gain, long_taps, cotangent):
    d = in_proj.shape[0]
    n_tp = d // C
    w = jnp.transpose(in_proj, (1, 0, 2))
    staps = jnp.transpose(short_taps, (1, 0, 2))
    taps = long_taps.astype(F32).T
    zeros = jnp.zeros((GROUP, LTAPS), F32)
    hfwd = jnp.concatenate([taps, zeros], axis=1).reshape(GROUP, 1, 2 * LTAPS)
    hrev = jnp.concatenate([zeros[:, :1], taps[:, ::-1], zeros[:, 1:]], axis=1).reshape(GROUP, 1, 2 * LTAPS)
    vm = pltpu.VMEM
    sem = pltpu.SemaphoreType.DMA
    scratch = [
        vm((n_tp, T, C), BF16), vm((n_tp, T, C), BF16), vm((3, d, C), BF16), vm((C, d), BF16),
        vm((3, T + 8, C), F32), vm((3, T, C), F32), vm((T, C), F32), vm((T, C), F32),
        vm((T, C), BF16), vm((C, T), BF16), vm((3, T, C), BF16),
        vm((NT + 1, C, LTAPS), BF16), vm((NT + 1, C, LTAPS), BF16), vm((NT, C, LTAPS), F32),
        vm((2, 3, 16, C), BF16), vm((2, 3, 16, C), BF16), vm((2, C, LTAPS), BF16),
        vm((GROUP, 1, LTAPS), F32), vm((7, GROUP, 1, LTAPS), F32),
        vm((1, C, 2 * C), F32), vm((T, C), BF16), vm((T, C), BF16),
        vm((8, 2, HALF, C), BF16), vm((8, 2, HALF, C), BF16), vm((8, 2, HALF, C), BF16),
        vm((2, 6, HALF, C), BF16), vm((2, 6, HALF, C), BF16), vm((2, 6, HALF, C), BF16),
        vm((2, HALF, C), BF16), vm((2, HALF, C), BF16), vm((2, HALF, C), BF16),
        vm((2, 6, 3, C, C), BF16), vm((2, 6, 3, C, C), BF16), vm((2, 3, C, C), BF16), vm((2, 3, C, C), BF16),
        vm((2, 6, 1, C, C), BF16), vm((2, 6, 1, C, C), BF16), vm((2, 1, C, C), BF16), vm((2, 1, C, C), BF16),
        sem((17,)), sem((17,)), sem((17,)), sem((17,)),
        sem((8,)), sem((8,)), sem((8,)), sem((8,)),
        sem((9,)), sem((9,)), sem((9,)), sem((9,)),
        sem((9,)), sem((9,)), sem((9,)), sem((9,)),
        sem((4,)), sem((4,)), sem((7,)), sem((7,)), sem((9,)),
    ]
    hbm = pl.BlockSpec(memory_space=pl.ANY)
    vmem = pl.BlockSpec(memory_space=pltpu.VMEM)
    layer_out, grad_inputs, grad_in, grad_out, tap_rows = pl.pallas_call(
        body,
        out_shape=[
            jax.ShapeDtypeStruct((T, C), BF16),
            jax.ShapeDtypeStruct((T, C), BF16),
            jax.ShapeDtypeStruct((3, 2 * C, C), F32),
            jax.ShapeDtypeStruct((C, 2 * C), F32),
            jax.ShapeDtypeStruct((GROUP, 1, LTAPS), F32),
        ],
        in_specs=[hbm, hbm, hbm, hbm, vmem, vmem, vmem, vmem],
        out_specs=[hbm] * 5,
        scratch_shapes=scratch,
        compiler_params=pltpu.CompilerParams(
            collective_id=0, has_side_effects=True, vmem_limit_bytes=67043328
        ),
    )(inputs, cotangent, w, out_proj, staps, skip_gain.reshape(1, C), hrev, hfwd)
    grad_taps = tap_rows.reshape(GROUP, LTAPS).T
    return (layer_out, grad_inputs, jnp.transpose(grad_in, (1, 0, 2)), grad_out, grad_taps)


def solution(mesh):
    placed = (
        P("ctx", "tp"),
        P(None, None, "tp"),
        P("tp", None),
        P(None, None, "tp"),
        P("tp"),
        P(None, "tp"),
        P("ctx", "tp"),
    )
    return jax.shard_map(
        local,
        mesh=mesh,
        in_specs=placed,
        out_specs=(
            P("ctx", "tp"),
            P("ctx", "tp"),
            P("ctx", None, "tp"),
            P("tp", "ctx"),
            P(None, "tp"),
        ),
        check_vma=False,
    )
```

```python
import jax
import jax.numpy as jnp
from jax import lax
from jax.experimental import pallas as pl
from jax.experimental.pallas import tpu as pltpu
from jax.sharding import PartitionSpec as P

GROUP = 16
LTAPS = 128
STAPS = 7
MESH = pl.DeviceIdType.MESH
F32 = jnp.float32
BF16 = jnp.bfloat16
T = 768
C = 256
NT = T // LTAPS
HALF = T // 2


def dot(a, b, dims=((1,), (0,))):
    return lax.dot_general(a, b, (dims, ((), ())), preferred_element_type=F32)


def remote(src, dst, send, recv, where):
    return pltpu.make_async_remote_copy(
        src_ref=src, dst_ref=dst, send_sem=send, recv_sem=recv, device_id=where, device_id_type=MESH
    )


class Gather:
    def __init__(self, src, buf, send, recv, z, h, k):
        self.src, self.buf = src, buf
        zp, zm, zo = lax.rem(z + 1, 4), lax.rem(z + 3, 4), lax.rem(z + 2, 4)

        def at(zz, hh, kk):
            return zz * 4 + hh * 2 + kk

        g, q = 1 - h, 1 - k
        plus, minus = {"tp": at(zp, h, k)}, {"tp": at(zm, h, k)}
        side, mate = {"tp": at(z, g, k)}, {"tp": at(z, h, q)}
        own = at(z, h, k)
        first, second = pl.ds(0, HALF), pl.ds(HALF, HALF)
        whole = pl.ds(0, T)
        plan = [
            (own, whole, plus),
            (own, whole, minus),
            (own, whole, side),
            (own, whole, mate),
            (at(z, g, k), whole, plus),
            (at(z, g, k), whole, minus),
            (at(z, g, k), whole, mate),
            (at(zm, h, k), first, plus),
            (at(zp, h, k), second, minus),
            (at(zm, h, k), whole, mate),
            (at(zp, h, k), whole, mate),
            (at(zm, g, k), first, plus),
            (at(zp, g, k), second, minus),
            (at(zm, g, k), whole, mate),
            (at(zp, g, k), whole, mate),
            (at(zo, h, k), whole, mate),
            (at(zo, g, k), whole, mate),
        ]
        self.copies = []
        for i, (slot, rows, where) in enumerate(plan):
            source = src if i < 4 else buf.at[slot, rows]
            self.copies.append(remote(source, buf.at[slot, rows], send.at[i], recv.at[i], where))
        self.groups = [
            (own, at(z, h, q)),
            (at(zm, h, k), at(zp, h, k)),
            (at(zm, h, q), at(zp, h, q)),
            (at(z, g, k), at(z, g, q)),
            (at(zm, g, k), at(zp, g, k)),
            (at(zm, g, q), at(zp, g, q)),
            (at(zo, h, k), at(zo, h, q)),
            (at(zo, g, k), at(zo, g, q)),
        ]

    def start(self, *which):
        for i in which:
            self.copies[i].start()

    def wait(self, *which):
        for i in which:
            self.copies[i].wait_recv()

    def drain(self):
        for copy in self.copies:
            copy.wait_send()


class Ring:
    def __init__(self, out, inn, side_out, side_in, send, recv, plus, minus, side, part):
        self.out, self.inn, self.side_out, self.side_in = out, inn, side_out, side_in
        self.part = part
        self.copies = []
        for kind in range(out.shape[0]):
            for i, (low, size, where) in enumerate([(0, 1, plus), (1, 1, minus), (2, 2, plus), (4, 2, minus)]):
                span = pl.ds(low, size)
                self.copies.append(
                    remote(out.at[kind, span], inn.at[kind, span], send.at[kind * 4 + i], recv.at[kind * 4 + i], where)
                )
        if side is not None:
            self.copies.append(remote(side_out, side_in, send.at[8], recv.at[8], side))

    def first(self, kind):
        for half in range(2):
            self.part("o", kind, half, [], self.out.at[kind, half])
            self.copies[kind * 4 + half].start()

    def second(self, kind):
        o, r = self.out, self.inn
        self.copies[kind * 4].wait_recv()
        self.part("p", kind, 0, [r.at[kind, 0]], o.at[kind, 2])
        self.part("p", kind, 1, [], o.at[kind, 3])
        self.copies[kind * 4 + 2].start()
        self.copies[kind * 4 + 1].wait_recv()
        self.part("m", kind, 0, [], o.at[kind, 4])
        self.part("m", kind, 1, [r.at[kind, 1]], o.at[kind, 5])
        self.copies[kind * 4 + 3].start()

    def third(self):
        r = self.inn
        self.copies[6].wait_recv()
        self.copies[7].wait_recv()
        for half in range(2):
            self.part("c", 1, half, [r.at[1, 2 + half], r.at[1, 4 + half]], self.side_out.at[half])
        self.copies[8].start()

    def last(self, targets):
        r = self.inn
        self.copies[2].wait_recv()
        self.copies[3].wait_recv()
        if self.side_in is not None:
            self.copies[8].wait_recv()
        for half in range(2):
            extra = [] if self.side_in is None else [self.side_in.at[half]]
            self.part("c", 0, half, [r.at[0, 2 + half], r.at[0, 4 + half]] + extra, targets[half])

    def sent(self, *which):
        for i in which:
            self.copies[i].wait_send()

    def drain(self):
        for copy in self.copies:
            copy.wait_send()


def body(
    inputs_ref, cot_ref, w_hbm, op_hbm, staps_ref, skip_ref, hrev_ref, hfwd_ref,
    lo_out, gi_out, gin_out, gout_out, taps_out,
    X, Y, W, OP, PF, QKV, WAVE, GF, FIL, FT, GM, GT, GWT, TT, HS, HR, HT, TG, TGR, GOS, LOS, GIS,
    YS, YR, BS, BR,
    SP, LRP, GRP, S, LR, GR, SY, LRY, GRY, CS, CR, CSY, CRY, OS, OR, OSY, ORY,
    xs, xr, ys, yr, lps, lpr, gps, gpr, ls, lr, gs, gr, cs, cr, os_, or_, hs, hr, ts, tr, loc, fs, fr, bs, br,
):
    ctx = lax.axis_index("ctx")
    me = lax.axis_index("tp")
    z, h, k = me // 4, lax.rem(me // 2, 2), lax.rem(me, 2)
    l, x = ctx // 4, lax.rem(ctx, 4)

    def at(zz, hh, kk):
        return zz * 4 + hh * 2 + kk

    zp, zm, zo = lax.rem(z + 1, 4), lax.rem(z + 3, 4), lax.rem(z + 2, 4)
    xp, xm, xo = lax.rem(x + 1, 4), lax.rem(x + 3, 4), lax.rem(x + 2, 4)
    mate = {"tp": at(z, h, 1 - k)}

    barrier = pltpu.get_barrier_semaphore()
    peers = [{"tp": at(zp, h, k)}, {"tp": at(zm, h, k)}, {"tp": at(z, 1 - h, k)}, mate]
    peers += [{"ctx": lax.rem(ctx + i, 8)} for i in range(1, 8)]
    for peer in peers:
        pl.semaphore_signal(barrier, inc=1, device_id=peer, device_id_type=MESH)
    pl.semaphore_wait(barrier, len(peers))

    gx = Gather(inputs_ref, X, xs, xr, z, h, k)
    gy = Gather(cot_ref, Y, ys, yr, z, h, k)
    gx.start(2, 0, 1, 3)
    gy.start(2)
    loads = [
        pltpu.make_async_copy(inputs_ref, X.at[me], loc.at[0]),
        pltpu.make_async_copy(w_hbm, W, loc.at[1]),
        pltpu.make_async_copy(op_hbm, OP, loc.at[2]),
        pltpu.make_async_copy(cot_ref, Y.at[me], loc.at[3]),
    ]
    for load in loads:
        load.start()

    def project(index, fresh=False):
        a, b = gx.groups[index]

        def one(s, _):
            for at_half in range(2):
                rows = pl.ds(at_half * HALF, HALF)
                to = pl.ds(8 + at_half * HALF, HALF)
                total = dot(X[a, rows], W[s, pl.ds(pl.multiple_of(a * C, C), C), :])
                total = total + dot(X[b, rows], W[s, pl.ds(pl.multiple_of(b * C, C), C), :])
                PF[s, to, :] = total if fresh else PF[s, to, :] + total
            return 0

        lax.fori_loop(0, 3, one, 0)

    loads[0].wait()
    loads[1].wait()
    gx.wait(3)
    project(0, True)
    gx.wait(0)
    gx.start(7, 9)
    gx.wait(1)
    gx.start(8, 10)
    gy.start(0, 1, 3)
    project(1)
    gx.wait(9, 10)
    project(2)
    gx.wait(7, 8)
    gx.start(15)
    gx.wait(2)
    gx.start(4, 5, 6)
    gx.wait(15)
    project(6)
    gx.wait(6)
    project(3)
    gx.wait(4)
    gx.start(11, 13)
    gx.wait(5)
    gx.start(12, 14)
    gy.wait(0, 1)
    gy.start(7, 9, 8, 10)
    project(4)
    gy.wait(2)
    gy.start(4, 5, 6)
    gx.wait(13, 14)
    project(5)
    gx.wait(11, 12)
    gx.start(16)
    gx.wait(16)
    project(7)

    def round_rows(i, _):
        s, r = i // NT, lax.rem(i, NT)
        rows = pl.ds(pl.multiple_of(8 + r * LTAPS, 8), LTAPS)
        PF[s, rows, :] = PF[s, rows, :].astype(BF16).astype(F32)
        return 0

    nxt, prv = {"ctx": lax.rem(ctx + 1, 8)}, {"ctx": lax.rem(ctx + 7, 8)}
    for s in range(3):
        HS[0, s] = PF[s, T - 8 : T + 8, :].astype(BF16)
    halo0 = remote(HS.at[0], HR.at[0], hs.at[0], hr.at[0], nxt)
    halo0.start()
    lax.fori_loop(0, 3 * NT, round_rows, 0)
    halo0.wait_recv()
    begins, ends = ctx == 0, ctx == 7
    for s in range(3):
        tail = HR[0, s].astype(F32)[8:16]
        PF[s, 0:8, :] = jnp.where(begins, 0.0, tail)

    def short_forward(i, _):
        s, r = i // NT, lax.rem(i, NT)
        window = PF[s, pl.ds(pl.multiple_of(r * LTAPS, 8), LTAPS + 8), :]
        total = staps_ref[s, 0:1, :] * window[8:]
        for j in range(1, STAPS):
            total = total + staps_ref[s, j : j + 1, :] * pltpu.roll(window, j, 0)[8:]
        QKV[s, pl.ds(pl.multiple_of(r * LTAPS, LTAPS), LTAPS), :] = total
        return 0

    lax.fori_loop(0, 3 * NT, short_forward, 0)

    def tile_rows(n):
        return pl.ds(pl.multiple_of(n * LTAPS, LTAPS), LTAPS)

    def gated_tile(n):
        return (QKV[1, tile_rows(n), :] * QKV[2, tile_rows(n), :]).astype(BF16).astype(F32)

    def put_gated(n, _):
        GT[n + 1] = gated_tile(n).T.astype(BF16)
        return 0

    lax.fori_loop(0, NT, put_gated, 0)
    halo1 = remote(GT.at[NT], HT.at[0], hs.at[1], hr.at[1], nxt)
    halo1.start()
    gy.wait(7, 8)
    gy.start(15)
    halo1.wait_recv()
    GT[0] = jnp.where(begins, 0.0, HT[0].astype(F32)).astype(BF16)

    def windows(ref, rows):
        return jnp.concatenate(
            [jnp.concatenate([ref[n, rows, :], ref[n + 1, rows, :]], axis=1) for n in range(NT)], axis=0
        )

    def band_of(ref, g):
        spread = jnp.broadcast_to(ref[g], (LTAPS, 2 * LTAPS))
        return pltpu.roll(spread, 0, 1, stride=1, stride_axis=0).astype(BF16)

    def convolve(g, _):
        rows = pl.ds(pl.multiple_of(g * GROUP, GROUP), GROUP)
        got = dot(windows(GT, rows), band_of(hrev_ref, g), ((1,), (1,)))
        for n in range(NT):
            TT[n, rows, :] = got[n * GROUP : (n + 1) * GROUP]
        return 0

    lax.fori_loop(0, GROUP, convolve, 0)
    gy.wait(4)
    gy.start(11, 13)
    gy.wait(5)
    gy.start(12, 14)

    for n in range(NT):
        rows = pl.ds(n * LTAPS, LTAPS)
        wave = TT[n].T + skip_ref[...] * gated_tile(n)
        WAVE[rows, :] = wave
        fil = (QKV[0, rows, :] * wave).astype(BF16)
        FIL[rows, :] = fil
        FT[:, rows] = fil.astype(F32).T.astype(BF16)

    def lo_part(slot, half):
        return dot(FIL[pl.ds(half * HALF, HALF), :], OP[:, pl.ds(pl.multiple_of(slot * C, C), C)])

    def gi_part(slot, half):
        rows = pl.ds(half * HALF, HALF)
        picked = pl.ds(pl.multiple_of(slot * C, C), C)
        total = dot(GM[0, rows, :], W[0, picked, :], ((1,), (1,)))
        total = total + dot(GM[1, rows, :], W[1, picked, :], ((1,), (1,)))
        return total + dot(GM[2, rows, :], W[2, picked, :], ((1,), (1,)))

    def for_mate(part, pairs):
        for index, pair in enumerate(pairs):
            def one(half, _, index=index):
                i = index
                zz, hh = (zo, zp, zm, z)[i // 2], (1 - h, h)[i % 2]
                SP[i, half] = part(at(zz, hh, 1 - k), half).astype(BF16)
                return 0

            lax.fori_loop(0, 2, one, 0)
            pair.start()

    def mate_pairs(into, send, recv):
        return [remote(SP.at[i], into.at[i], send.at[i], recv.at[i], mate) for i in range(8)]

    def tp_ring(part, from_mate, pairs, inn, side_in, send, recv):
        def term(name, kind, half, extra, target):
            place = {"o": 0, "p": 1, "m": 2, "c": 3}[name]
            index = place * 2 + (0 if kind == 1 else 1)
            if half == 0:
                pairs[index].wait_recv()
            zz = (zo, zp, zm, z)[place]
            hh = 1 - h if kind == 1 else h
            total = part(at(zz, hh, k), half) + from_mate[index, half].astype(F32)
            for ref in extra:
                total = total + ref[...].astype(F32)
            target[...] = total.astype(target.dtype)

        return Ring(
            S, inn, SY, side_in, send, recv,
            {"tp": at(zp, h, k)}, {"tp": at(zm, h, k)}, {"tp": at(z, 1 - h, k)}, term,
        )

    def ctx_ring(fill, out, inn, side_out, side_in, send, recv):
        def term(name, kind, half, extra, target):
            xx = {"o": xo, "p": xp, "m": xm, "c": x}[name]
            ll = 1 - l if kind == 1 else l
            fill((ll * 4 + xx) * 2 + half, half, extra, target)

        return Ring(
            out, inn, side_out, side_in, send, recv,
            {"ctx": l * 4 + xp}, {"ctx": l * 4 + xm}, {"ctx": (1 - l) * 4 + x}, term,
        )

    loads[2].wait()
    lo_pairs = mate_pairs(LRP, lps, lpr)
    for_mate(lo_part, lo_pairs)

    def filter_grad(index, fresh=False):
        a, b = gy.groups[index]

        def one(i, _):
            rows = pl.ds(pl.multiple_of(i * HALF, HALF), HALF)
            total = dot(Y[a, rows, :], OP[:, pl.ds(pl.multiple_of(a * C, C), C)], ((1,), (1,)))
            total = total + dot(Y[b, rows, :], OP[:, pl.ds(pl.multiple_of(b * C, C), C)], ((1,), (1,)))
            GF[rows, :] = total if fresh else GF[rows, :] + total
            return 0

        lax.fori_loop(0, 2, one, 0)

    loads[3].wait()
    gy.wait(3)
    filter_grad(0, True)
    filter_grad(1)
    gy.wait(9, 10)
    filter_grad(2)
    gy.wait(6)
    filter_grad(3)
    filter_grad(4)
    gy.wait(15)
    filter_grad(6)
    gy.wait(13, 14)
    filter_grad(5)
    lo = tp_ring(lo_part, LRP, lo_pairs, LR, LRY, ls, lr)
    lo.first(1)
    lo.first(0)
    gy.wait(11, 12)
    gy.start(16)
    gy.wait(16)
    filter_grad(7)

    def put_grad_wave(n, _):
        rows = tile_rows(n)
        GWT[n] = (GF[rows, :] * QKV[0, rows, :]).astype(BF16).astype(F32).T.astype(BF16)
        return 0

    lax.fori_loop(0, NT, put_grad_wave, 0)
    halo2 = remote(GWT.at[0], HT.at[1], hs.at[2], hr.at[2], prv)
    halo2.start()

    def go_fill(slot, half, extra, target):
        total = dot(FT[...], Y[slot])
        for ref in extra:
            total = total + ref[0].astype(F32)
        target[0] = total.astype(target.dtype)

    go = ctx_ring(go_fill, OS, OR, OSY, ORY, os_, or_)
    go.first(1)
    go.first(0)

    halo2.wait_recv()
    GWT[NT] = jnp.where(ends, 0.0, HT[1].astype(F32)).astype(BF16)

    def convolve_back(g, _):
        rows = pl.ds(pl.multiple_of(g * GROUP, GROUP), GROUP)
        got = dot(windows(GWT, rows), band_of(hfwd_ref, g), ((1,), (1,)))
        for n in range(NT):
            TT[n, rows, :] = got[n * GROUP : (n + 1) * GROUP]
        return 0

    lax.fori_loop(0, GROUP, convolve_back, 0)

    def to_mixed(n, _):
        rows = tile_rows(n)
        gf, q = GF[rows, :], QKV[0, rows, :]
        gw = (gf * q).astype(BF16).astype(F32)
        gg = TT[n].T + skip_ref[...] * gw
        PF[0, rows, :] = (gf * WAVE[rows, :]).astype(BF16).astype(F32)
        PF[1, rows, :] = (gg * QKV[2, rows, :]).astype(BF16).astype(F32)
        PF[2, rows, :] = (gg * QKV[1, rows, :]).astype(BF16).astype(F32)
        return 0

    lax.fori_loop(0, NT, to_mixed, 0)
    for s in range(3):
        HS[1, s] = PF[s, 0:16, :].astype(BF16)
    halo3 = remote(HS.at[1], HR.at[1], hs.at[3], hr.at[3], prv)
    halo3.start()
    lo.second(1)
    lo.second(0)

    def correlate(g, _):
        rows = pl.ds(pl.multiple_of(g * GROUP, GROUP), GROUP)
        now = jnp.concatenate([GWT[n, rows, :] for n in range(NT)], axis=0)
        across = lax.broadcasted_iota(jnp.int32, (LTAPS, LTAPS), 0) + lax.broadcasted_iota(jnp.int32, (LTAPS, LTAPS), 1)
        mirror = jnp.where(across == LTAPS - 1, 1.0, 0.0).astype(BF16)
        tiles = [dot(GT[n, rows, :], mirror).astype(BF16) for n in range(NT + 1)]
        seen = jnp.concatenate(
            [jnp.concatenate([tiles[n + 1], tiles[n]], axis=1) for n in range(NT)], axis=0
        )
        pairs = dot(now, seen, ((0,), (0,)))
        TG[g] = jnp.sum(pltpu.roll(pairs, LTAPS + 1, 1, stride=1, stride_axis=0)[:, :LTAPS], axis=0, keepdims=True)
        return 0

    go.second(1)
    halo3.wait_recv()
    for s in range(3):
        head = HR[1, s].astype(F32)[0:8]
        PF[s, T : T + 8, :] = jnp.where(ends, 0.0, head)

    def short_backward(i, _):
        s, r = i // NT, lax.rem(i, NT)
        window = PF[s, pl.ds(pl.multiple_of(r * LTAPS, 8), LTAPS + 8), :]
        total = staps_ref[s, 0:1, :] * window[:LTAPS]
        for j in range(1, STAPS):
            total = total + staps_ref[s, j : j + 1, :] * pltpu.roll(window, LTAPS + 8 - j, 0)[:LTAPS]
        GM[s, pl.ds(pl.multiple_of(r * LTAPS, LTAPS), LTAPS), :] = total.astype(BF16)
        return 0

    lax.fori_loop(0, 3 * NT, short_backward, 0)

    def gin_fill(slot, half, extra, target):
        flipped = X[slot]

        def one(s, _):
            total = dot(flipped, GM[s], ((0,), (0,)))
            for ref in extra:
                total = total + ref[s].astype(F32)
            target[s] = total.astype(target.dtype)
            return 0

        lax.fori_loop(0, 2, one, 0)

    gin = ctx_ring(gin_fill, CS, CR, CSY, CRY, cs, cr)
    flat_pairs = [remote(YS.at[i], YR.at[i], fs.at[i], fr.at[i], {"ctx": (1 - l) * 4 + x}) for i in range(4)]
    places = (xo, xp, xm, x)

    def flat_part(ll, i, half):
        return dot(X[(ll * 4 + places[i]) * 2 + half], GM[2], ((0,), (0,)))

    def flat_term(name, kind, half, extra, target):
        i = {"o": 0, "p": 1, "m": 2, "c": 3}[name]
        if half == 0:
            flat_pairs[i].wait_recv()
        total = flat_part(l, i, half) + YR[i, half].astype(F32)
        for ref in extra:
            total = total + ref[...].astype(F32)
        target[...] = total.astype(target.dtype)

    flat = Ring(BS, BR, None, None, bs, br, {"ctx": l * 4 + xp}, {"ctx": l * 4 + xm}, None, flat_term)
    gin.first(1)
    for i in range(4):
        def one(half, _, i=i):
            YS[i, half] = flat_part(1 - l, i, half).astype(BF16)
            return 0

        lax.fori_loop(0, 2, one, 0)
        flat_pairs[i].start()
    gin.first(0)
    go.second(0)
    for pair in lo_pairs:
        pair.wait_send()
    gi_pairs = mate_pairs(GRP, gps, gpr)
    for_mate(gi_part, gi_pairs)
    lo.third()
    go.third()
    gi = tp_ring(gi_part, GRP, gi_pairs, GR, GRY, gs, gr)
    lo.sent(4, 5)
    gi.first(1)
    lo.sent(0, 1)
    gi.first(0)
    flat.first(0)
    gin.second(1)
    lo.sent(6, 7)
    gi.second(1)
    flat.second(0)
    gin.second(0)
    lo.sent(2, 3)
    gi.second(0)
    lax.fori_loop(0, GROUP, correlate, 0)
    tap_sends = []
    for i in range(7):
        tap_sends.append(remote(TG, TGR.at[i], ts.at[i], tr.at[i], {"ctx": lax.rem(ctx + i + 1, 8)}))
        tap_sends[-1].start()
    lo.sent(8)
    gi.third()
    lo.last([LOS.at[pl.ds(0, HALF)], LOS.at[pl.ds(HALF, HALF)]])
    lo_store = pltpu.make_async_copy(LOS, lo_out, loc.at[4])
    lo_store.start()
    go.last([GOS.at[:, :, pl.ds(0, C)], GOS.at[:, :, pl.ds(C, C)]])
    go_store = pltpu.make_async_copy(GOS.at[0], gout_out, loc.at[5])
    go_store.start()
    gin.third()
    total = TG[...]
    for i in range(7):
        tap_sends[i].wait_recv()
        total = total + TGR[i]
    for i in range(7):
        tap_sends[i].wait_send()
    TG[...] = total
    tap_store = pltpu.make_async_copy(TG, taps_out, loc.at[6])
    tap_store.start()
    gi.last([GIS.at[pl.ds(0, HALF)], GIS.at[pl.ds(HALF, HALF)]])
    gi_store = pltpu.make_async_copy(GIS, gi_out, loc.at[7])
    gi_store.start()
    flat.last([PF.at[2, pl.ds(0, C)], PF.at[2, pl.ds(C, C)]])
    gin.last([PF.at[:, pl.ds(0, C)], PF.at[:, pl.ds(C, C)]])
    gin_store = pltpu.make_async_copy(PF.at[:, pl.ds(0, 2 * C)], gin_out, loc.at[8])
    gin_store.start()

    gx.drain()
    gy.drain()
    go.drain()
    gi.drain()
    gin.drain()
    flat.drain()
    for pair in flat_pairs:
        pair.wait_send()
    for pair in gi_pairs:
        pair.wait_send()
    for copy in (halo0, halo1, halo2, halo3):
        copy.wait_send()
    for store in (lo_store, go_store, tap_store, gi_store, gin_store):
        store.wait()


def local(inputs, in_proj, out_proj, short_taps, skip_gain, long_taps, cotangent):
    d = in_proj.shape[0]
    n_tp = d // C
    w = jnp.transpose(in_proj, (1, 0, 2))
    staps = jnp.transpose(short_taps, (1, 0, 2))
    taps = long_taps.astype(F32).T
    zeros = jnp.zeros((GROUP, LTAPS), F32)
    hfwd = jnp.concatenate([taps, zeros], axis=1).reshape(GROUP, 1, 2 * LTAPS)
    hrev = jnp.concatenate([zeros[:, :1], taps[:, ::-1], zeros[:, 1:]], axis=1).reshape(GROUP, 1, 2 * LTAPS)
    vm = pltpu.VMEM
    sem = pltpu.SemaphoreType.DMA
    scratch = [
        vm((n_tp, T, C), BF16), vm((n_tp, T, C), BF16), vm((3, d, C), BF16), vm((C, d), BF16),
        vm((3, T + 8, C), F32), vm((3, T, C), F32), vm((T, C), F32), vm((T, C), F32),
        vm((T, C), BF16), vm((C, T), BF16), vm((3, T, C), BF16),
        vm((NT + 1, C, LTAPS), BF16), vm((NT + 1, C, LTAPS), BF16), vm((NT, C, LTAPS), F32),
        vm((2, 3, 16, C), BF16), vm((2, 3, 16, C), BF16), vm((2, C, LTAPS), BF16),
        vm((GROUP, 1, LTAPS), F32), vm((7, GROUP, 1, LTAPS), F32),
        vm((1, C, 2 * C), F32), vm((T, C), BF16), vm((T, C), BF16),
        vm((4, 2, C, C), BF16), vm((4, 2, C, C), BF16), vm((1, 6, C, C), BF16), vm((1, 6, C, C), BF16),
        vm((8, 2, HALF, C), BF16), vm((8, 2, HALF, C), BF16), vm((8, 2, HALF, C), BF16),
        vm((2, 6, HALF, C), BF16), vm((2, 6, HALF, C), BF16), vm((2, 6, HALF, C), BF16),
        vm((2, HALF, C), BF16), vm((2, HALF, C), BF16), vm((2, HALF, C), BF16),
        vm((2, 6, 2, C, C), BF16), vm((2, 6, 2, C, C), BF16), vm((2, 2, C, C), BF16), vm((2, 2, C, C), BF16),
        vm((2, 6, 1, C, C), BF16), vm((2, 6, 1, C, C), BF16), vm((2, 1, C, C), BF16), vm((2, 1, C, C), BF16),
        sem((17,)), sem((17,)), sem((17,)), sem((17,)),
        sem((8,)), sem((8,)), sem((8,)), sem((8,)),
        sem((9,)), sem((9,)), sem((9,)), sem((9,)),
        sem((9,)), sem((9,)), sem((9,)), sem((9,)),
        sem((4,)), sem((4,)), sem((7,)), sem((7,)), sem((9,)),
        sem((4,)), sem((4,)), sem((4,)), sem((4,)),
    ]
    hbm = pl.BlockSpec(memory_space=pl.ANY)
    vmem = pl.BlockSpec(memory_space=pltpu.VMEM)
    layer_out, grad_inputs, grad_in, grad_out, tap_rows = pl.pallas_call(
        body,
        out_shape=[
            jax.ShapeDtypeStruct((T, C), BF16),
            jax.ShapeDtypeStruct((T, C), BF16),
            jax.ShapeDtypeStruct((3, 2 * C, C), F32),
            jax.ShapeDtypeStruct((C, 2 * C), F32),
            jax.ShapeDtypeStruct((GROUP, 1, LTAPS), F32),
        ],
        in_specs=[hbm, hbm, hbm, hbm, vmem, vmem, vmem, vmem],
        out_specs=[hbm] * 5,
        scratch_shapes=scratch,
        compiler_params=pltpu.CompilerParams(
            collective_id=0, has_side_effects=True, vmem_limit_bytes=67043328
        ),
    )(inputs, cotangent, w, out_proj, staps, skip_gain.reshape(1, C), hrev, hfwd)
    grad_taps = tap_rows.reshape(GROUP, LTAPS).T
    return (layer_out, grad_inputs, jnp.transpose(grad_in, (1, 0, 2)), grad_out, grad_taps)


def solution(mesh):
    placed = (
        P("ctx", "tp"),
        P(None, None, "tp"),
        P("tp", None),
        P(None, None, "tp"),
        P("tp"),
        P(None, "tp"),
        P("ctx", "tp"),
    )
    return jax.shard_map(
        local,
        mesh=mesh,
        in_specs=placed,
        out_specs=(
            P("ctx", "tp"),
            P("ctx", "tp"),
            P("ctx", None, "tp"),
            P("tp", "ctx"),
            P(None, "tp"),
        ),
        check_vma=False,
    )
```
